128 devices in a mesh: own: 4 (over z), img: 32 (over x, y, core).
Axes of the slice: x: 4, y: 4, z: 4, core: 2. Of those that a mesh axis runs over, the one named last changes fastest.
Arguments:
- mask_field: bfloat16 [4096, 16384], P('own', 'img'), may hold values from -1 to 1
- target_field: bfloat16 [4096, 16384], P('own', 'img'), may hold values from 0 to 1
- occupancy: int32 [8, 32], replicated, may hold values 0 or 1
- kernels: float32 [2, 24, 32, 32], replicated, may hold values from -9 to 9
- weights: float32 [24], replicated, may hold values from 0.01 to 0.3
Outputs:
- gradient: float32 [4096, 16384], P('own', 'img')
The draws below stay inside these ranges and needn't reach their ends.
All inputs are finite; a program needn't handle non-finite values.
Results may differ from the reference program's by a relative error of at most 0.0072.
Values may be sent and summed in bfloat16 or wider, within the bound.
No kernel may reach another device: no remote copies, remote signals or barrier semaphores. Data moves between devices by JAX's collectives and lax.ppermute only.
A program may use at most 64 MiB of HBM per device.

```python
import math
import jax
import jax.numpy as jnp
from jax import lax

TILE = 512
AMBIT = 64
FREQ = 32
KERNELS = 24
PAD = 640
GY = 8
GX = 32
NY = 4096
NX = 16384


def with_ends(drawn, stream_key, smallest, largest):
    longest = drawn.shape.index(max(drawn.shape))
    spots = []
    for shift in (0, 1):
        where = [jax.random.randint(jax.random.fold_in(stream_key, axis), (), 0, length) for axis, length in enumerate(drawn.shape)]
        where[longest] = (where[longest] + shift) % drawn.shape[longest]
        spots.append(tuple(where))
    return drawn.at[spots[0]].set(smallest).at[spots[1]].set(largest)


def block_levels(rng, dims, pieces, low, largest):
    loudness = 1.0
    for dim, shards_of in pieces:
        steps = jax.random.uniform(jax.random.fold_in(jax.random.fold_in(rng, 6), dim), (shards_of,), jnp.float32, low / len(pieces), largest / len(pieces))
        loudness = loudness * jnp.repeat(jnp.exp(steps), dims[dim] // shards_of).reshape((-1,) + (1,) * (len(dims) - 1 - dim))
    return loudness


def normal_values(rng, extent, deviation, most, kind=jnp.bfloat16):
    drawn = deviation * jax.random.normal(rng, extent, jnp.float32)
    return jnp.clip(drawn, min=-most, max=most).astype(kind)


def setup_inputs(seed: int = 0) -> dict:
    key_of = jax.random.split(jax.random.key(seed), 6)
    mask_field = jnp.clip(jax.random.uniform(key_of[0], (NY, NX), jnp.float32, -1.0, 1.0) * block_levels(key_of[0], (NY, NX), ((0, 4), (1, 32)), -0.4, 0.0), -1.0, 1.0).astype(jnp.bfloat16)
    target_field = jnp.clip(1.0 * jax.random.uniform(key_of[1], (NY, NX), jnp.float32) ** block_levels(key_of[1], (NY, NX), ((0, 4), (1, 32)), -0.2, 0.2), 0.0, 1.0).astype(jnp.bfloat16)
    occupancy = with_ends((jax.random.randint(key_of[2], (GY, GX), 0, 5) < 2).astype(jnp.int32), jax.random.fold_in(key_of[2], 1), 0, 1)
    kernels = normal_values(key_of[3], (2, KERNELS, FREQ, FREQ), 1.5, 9.0, jnp.float32)
    weights = jnp.clip(jnp.exp(jax.random.uniform(key_of[4], (KERNELS,), jnp.float32, math.log(0.01), math.log(0.3))), 0.01, 0.3)
    return {"mask_field": mask_field, "target_field": target_field, "occupancy": occupancy, "kernels": kernels, "weights": weights}


STEEP = 2.0
THRESHOLD = 1.5
GAMMA = 0.25

def mixed_dot(left, right):
    return jnp.dot(left, right, preferred_element_type=jnp.float32)

def exact_dot(left, right):
    return jnp.dot(left, right, precision=lax.Precision.HIGHEST, preferred_element_type=jnp.float32)

def dft_tables(padded_len, core_len, ambit_len, freq_count):
    freqs = jnp.arange(freq_count, dtype=jnp.int32) - freq_count // 2
    pixels = jnp.arange(padded_len, dtype=jnp.int32)
    phase = jnp.mod(freqs[:, None] * pixels[None, :], padded_len).astype(jnp.float32) * (2.0 * math.pi / padded_len)
    fwd_cos = (jnp.cos(phase) / math.sqrt(padded_len)).astype(jnp.bfloat16)
    fwd_sin = (-jnp.sin(phase) / math.sqrt(padded_len)).astype(jnp.bfloat16)
    out_rows = jnp.arange(core_len, dtype=jnp.int32) + ambit_len
    back_phase = jnp.mod(out_rows[:, None] * freqs[None, :], padded_len).astype(jnp.float32) * (2.0 * math.pi / padded_len)
    inv_cos = (jnp.cos(back_phase) / math.sqrt(freq_count)).astype(jnp.bfloat16)
    inv_sin = (jnp.sin(back_phase) / math.sqrt(freq_count)).astype(jnp.bfloat16)
    return (fwd_cos, fwd_sin, inv_cos, inv_sin)

def tile_gradient(padded_tile, target_tile, kernels, weights, tables):
    fwd_cos, fwd_sin, inv_cos, inv_sin = tables
    back_cos = inv_cos.astype(jnp.float32)
    back_sin = inv_sin.astype(jnp.float32)
    upper_re = mixed_dot(fwd_cos, padded_tile).astype(jnp.bfloat16)
    upper_im = mixed_dot(fwd_sin, padded_tile).astype(jnp.bfloat16)
    spec_re = mixed_dot(upper_re, fwd_cos.T) - mixed_dot(upper_im, fwd_sin.T)
    spec_im = mixed_dot(upper_re, fwd_sin.T) + mixed_dot(upper_im, fwd_cos.T)

    def field(which):
        kern_re = kernels[0, which]
        kern_im = kernels[1, which]
        prod_re = kern_re * spec_re - kern_im * spec_im
        prod_im = kern_re * spec_im + kern_im * spec_re
        half_re = (exact_dot(prod_re, back_cos.T) - exact_dot(prod_im, back_sin.T)).astype(jnp.bfloat16)
        half_im = (exact_dot(prod_re, back_sin.T) + exact_dot(prod_im, back_cos.T)).astype(jnp.bfloat16)
        field_re = mixed_dot(inv_cos, half_re) - mixed_dot(inv_sin, half_im)
        field_im = mixed_dot(inv_cos, half_im) + mixed_dot(inv_sin, half_re)
        return (field_re, field_im)

    def add_intensity(which, total):
        field_re, field_im = field(which)
        return total + weights[which] * (field_re * field_re + field_im * field_im)
    intensity = lax.fori_loop(0, KERNELS, add_intensity, jnp.zeros((TILE, TILE), jnp.float32))
    resist = jax.nn.sigmoid(STEEP * (intensity - THRESHOLD))
    sens = 2.0 * (resist - target_tile.astype(jnp.float32)) * STEEP * resist * (1.0 - resist)

    def add_adjoint(which, spec_grad):
        kern_re = kernels[0, which]
        kern_im = kernels[1, which]
        field_re, field_im = field(which)
        factor = 2.0 * weights[which] * sens
        cot_re = (factor * field_re).astype(jnp.bfloat16)
        cot_im = (factor * field_im).astype(jnp.bfloat16)
        dp_re = mixed_dot(inv_cos.T, cot_re) + mixed_dot(inv_sin.T, cot_im)
        dp_im = mixed_dot(inv_cos.T, cot_im) - mixed_dot(inv_sin.T, cot_re)
        ds_re = exact_dot(dp_re, back_cos) + exact_dot(dp_im, back_sin)
        ds_im = exact_dot(dp_im, back_cos) - exact_dot(dp_re, back_sin)
        grad_re, grad_im = spec_grad
        return (grad_re + kern_re * ds_re + kern_im * ds_im, grad_im + kern_re * ds_im - kern_im * ds_re)
    zero_spec = jnp.zeros((FREQ, FREQ), jnp.float32)
    grad_re, grad_im = lax.fori_loop(0, KERNELS, add_adjoint, (zero_spec, zero_spec))
    fwd_cos_wide = fwd_cos.astype(jnp.float32)
    fwd_sin_wide = fwd_sin.astype(jnp.float32)
    du_re = (exact_dot(grad_re, fwd_cos_wide) + exact_dot(grad_im, fwd_sin_wide)).astype(jnp.bfloat16)
    du_im = (exact_dot(grad_im, fwd_cos_wide) - exact_dot(grad_re, fwd_sin_wide)).astype(jnp.bfloat16)
    return mixed_dot(fwd_cos.T, du_re) + mixed_dot(fwd_sin.T, du_im)

def reference(mask_field, target_field, occupancy, kernels, weights):
    tables = dft_tables(PAD, TILE, AMBIT, FREQ)
    padded_field = jnp.pad(mask_field, AMBIT)
    total = jnp.zeros((NY + 2 * AMBIT, NX + 2 * AMBIT), jnp.float32)
    blank = jnp.zeros((PAD, PAD), jnp.float32)

    def visit(total, position):
        row_tile = position // GX
        col_tile = position % GX
        top = (row_tile * TILE).astype(jnp.int32)
        left = (col_tile * TILE).astype(jnp.int32)
        window = lax.dynamic_slice(padded_field, (top, left), (PAD, PAD))
        wanted = lax.dynamic_slice(target_field, (top, left), (TILE, TILE))
        flag = occupancy[row_tile, col_tile]
        contrib = lax.cond(flag > 0, lambda: tile_gradient(window, wanted, kernels, weights, tables), lambda: blank)
        contrib = lax.optimization_barrier(contrib.astype(jnp.bfloat16)).astype(jnp.float32)
        current = lax.dynamic_slice(total, (top, left), (PAD, PAD))
        return (lax.dynamic_update_slice(total, current + contrib, (top, left)), None)
    total, unused = lax.scan(visit, total, jnp.arange(GY * GX, dtype=jnp.int32))
    values = mask_field.astype(jnp.float32)
    penalty = GAMMA * 4.0 * values * (values * values - 1.0)
    return total[AMBIT:AMBIT + NY, AMBIT:AMBIT + NX] + penalty
```

```python
import jax
import jax.numpy as jnp
import numpy as np
from jax import lax
from jax.experimental import pallas as pl
from jax.experimental.pallas import tpu as pltpu
from jax.sharding import PartitionSpec as P

TILE = 512
AMBIT = 64
FREQ = 32
KERNELS = 24
PAD = 640
GRID = 64

STEEP = 2.0
THRESHOLD = 1.5
GAMMA = 0.25

BF = jnp.bfloat16
F32 = jnp.float32


def _bf(x):
    return np.asarray(x, np.float32).astype(BF)


def _hi_lo(x):
    hi = _bf(x)
    return hi, _bf(np.asarray(x, np.float64) - hi.astype(np.float64))


def _build_tables():
    f = np.arange(FREQ) - FREQ // 2
    ang = 2 * np.pi * ((f[:, None] * np.arange(PAD)[None]) % PAD) / PAD
    c = _bf(np.cos(ang) / np.sqrt(PAD)).astype(np.float64)
    s = _bf(-np.sin(ang) / np.sqrt(PAD)).astype(np.float64)

    height, width = 2 * TILE, TILE
    first = {0: AMBIT + TILE, 1: AMBIT, 2: AMBIT - TILE, 3: AMBIT - 2 * TILE}

    def rows_of(table, r):
        out = np.zeros((FREQ, height))
        y = np.arange(height) + first[r]
        ok = (y >= 0) & (y < PAD)
        out[:, ok] = table[:, y[ok]]
        return out

    fwd = np.concatenate(
        [rows_of(c, 0), rows_of(c, 3), rows_of(s, 0), rows_of(s, 3)]
        + [rows_of(c, 1), rows_of(c, 2), rows_of(s, 1), rows_of(s, 2)],
        0,
    )

    def cols_of(table, shift, lo, hi):
        out = np.zeros((FREQ, hi - lo))
        x = np.arange(lo, hi) + shift
        ok = (x >= 0) & (x < PAD)
        out[:, ok] = table[:, x[ok]]
        return out

    t = {"fwd": _bf(fwd), "bwd": _bf(fwd.T)}
    ranges = {"mid": (AMBIT, 0, width), "left": (AMBIT + TILE, 0, 128), "right": (AMBIT - TILE, width - 128, width)}
    for name, (shift, lo, hi) in ranges.items():
        cc, ss = cols_of(c, shift, lo, hi), cols_of(s, shift, lo, hi)
        re = np.concatenate([cc.T, ss.T], 1)
        im = np.concatenate([-ss.T, cc.T], 1)
        both = np.concatenate([re, im], 0)
        t["f_" + name] = _bf(np.concatenate([both, both], 1))
        dre, dim = np.concatenate([cc, ss], 0), np.concatenate([-ss, cc], 0)
        t["b_" + name] = _bf(np.concatenate([np.concatenate([dre, dre], 0), np.concatenate([dim, dim], 0)], 1))

    grid = np.arange(GRID) * (PAD // GRID)
    hang = 2 * np.pi * ((grid[:, None] * f[None]) % PAD) / PAD
    hc, hs = np.cos(hang) / np.sqrt(FREQ), np.sin(hang) / np.sqrt(FREQ)
    tp = np.concatenate(
        [
            np.concatenate([hc.T, hs.T, -hs.T, hc.T], 1),
            np.concatenate([-hs.T, hc.T, -hc.T, -hs.T], 1),
        ],
        0,
    )
    hi, lo = _hi_lo(tp)
    t["tp"] = np.concatenate([hi, hi, hi, hi, lo, lo], 0)
    hi, lo = _hi_lo(np.concatenate([hc, hs], 1))
    t["te"] = np.concatenate([hi, hi, lo], 1)
    t["tx"] = hi.T.copy()
    v1 = np.block([[hc, -hs], [hs, hc]])
    v2 = np.block([[-hs, -hc], [hc, -hs]])
    v = np.concatenate([v1, v2], 0)
    t["tv"] = _bf(np.concatenate([v, v[:, FREQ:], -v[:, :FREQ]], 1))

    n = np.arange(1 - FREQ, FREQ)
    y = np.arange(TILE) + AMBIT
    w = np.cos(2 * np.pi * ((y[:, None, None] - grid[None, :, None]) * n[None, None, :] % PAD) / PAD).sum(-1) / GRID
    hi, lo = _hi_lo(w)
    t["tz"] = np.concatenate([hi.T, hi.T, hi.T, hi.T, lo.T, lo.T], 0)
    t["tw"] = np.concatenate([hi, hi, lo], 1)
    t["ty"] = np.concatenate([hi, hi, lo, lo], 1)
    t["tg"] = np.concatenate([hi.T, lo.T], 0)
    return t


TABLES = _build_tables()


def _dot(a, b):
    return jnp.dot(a, b, preferred_element_type=F32)


def _split(x):
    hi = x.astype(BF)
    return hi, (x - hi.astype(F32)).astype(BF)


def _low_lanes(shape):
    return lax.broadcasted_iota(jnp.int32, shape, len(shape) - 1) < 64


def _forward_kernel(mask_ref, fwd_ref, mid_ref, left_ref, right_ref, own_ref, a_ref, b_ref, acc):
    acc[...] = _dot(fwd_ref[...], mask_ref[...]).astype(BF)
    odd = lax.rem(lax.axis_index("img"), 2) == 1

    def project(lo, hi, table):
        re03, im03 = acc[0:64, lo:hi], acc[64:128, lo:hi]
        re12, im12 = acc[128:192, lo:hi], acc[192:256, lo:hi]
        lhs = jnp.concatenate(
            [jnp.concatenate([re03, im03], 1), jnp.concatenate([re12, im12], 1)], 0
        )
        out = _dot(lhs, table[...])
        return jnp.where(_low_lanes((64, 128)), out[:64], out[64:])

    own_ref[...] = project(0, 512, mid_ref)
    left = project(0, 128, left_ref)
    right = project(384, 512, right_ref)
    a_ref[...] = jnp.where(odd, left, right)
    b_ref[...] = jnp.where(odd, right, left)


def _image_kernel(
    x_ref, ua_ref, ub_ref, kk_ref, target_ref, occ_ref,
    tp_ref, te_ref, tx_ref, tv_ref, tz_ref, tw_ref, ty_ref, tg_ref,
    out_ref, p_hi, p_lo, fields, xs, yb,
):
    band, col = lax.axis_index("own"), lax.axis_index("img")
    even = lax.rem(band, 2) == 0
    inner = (band == 1) | (band == 2)
    ua = ua_ref[...]
    ub = jnp.where(inner, ub_ref[...], 0.0)
    from_up = jnp.where(even, ub, ua)
    from_down = jnp.where(even, ua, ub)
    low = _low_lanes((FREQ, 128))
    lane = lax.broadcasted_iota(jnp.int32, (FREQ, 128), 1)

    kk = kk_ref[...]
    for t, extra in enumerate((from_up, from_down)):
        m = x_ref[t * FREQ : (t + 1) * FREQ, :]
        m = pltpu.roll(m, 64, 1) + extra
        dup = jnp.where(low, m, pltpu.roll(m, 64, 1))
        swapped = pltpu.roll(dup, 32, 1)
        swapped = jnp.where(lane < 96, -swapped, swapped)
        m4 = jnp.where(low, dup, swapped)
        prod = kk * m4[None]
        hi, lo = _split(prod.reshape(KERNELS * FREQ, 128))
        half = _dot(jnp.concatenate([hi, lo, hi], 1), tp_ref[...])
        hi, lo = _split(half)
        p_hi[t] = hi.reshape(KERNELS, FREQ, 256)
        p_lo[t] = lo.reshape(KERNELS, FREQ, 256)

    total = jnp.zeros((GRID, 256), F32)
    for k in range(KERNELS):
        def halves(ref):
            return jnp.concatenate(
                [
                    jnp.concatenate([ref[0, k, :, :128], ref[1, k, :, :128]], 1),
                    jnp.concatenate([ref[0, k, :, 128:], ref[1, k, :, 128:]], 1),
                ],
                0,
            )
        hi = halves(p_hi)
        e = _dot(te_ref[...], jnp.concatenate([hi, halves(p_lo), hi], 0))
        fields[k] = e
        total = total + e * e

    hi, lo = _split(jnp.concatenate([total[:, :128], total[:, 128:]], 0))
    z = _dot(jnp.concatenate([hi, lo, hi], 1), tz_ref[...])
    pulls = []
    rows = 128
    for t in range(2):
        hi, lo = _split(z[t * GRID : (t + 1) * GRID])
        stack = jnp.concatenate([hi, lo, hi], 0)
        for c in range(TILE // rows):
            at = c * rows
            intensity = _dot(tw_ref[at : at + rows], stack)
            th = jnp.tanh((0.5 * STEEP) * (intensity - THRESHOLD))
            wanted = target_ref[t * TILE + at : t * TILE + at + rows, :].astype(F32)
            sens = (0.5 * STEEP) * (0.5 + 0.5 * th - wanted) * (1.0 - th * th)
            y = _dot(sens.astype(BF), ty_ref[...])
            yb[at : at + rows, :] = (y[:, :128] + y[:, 128:]).astype(BF)
        g = _dot(tg_ref[...], yb[...])
        pulls.append(2.0 * (g[:GRID] + g[GRID:]))
    pull = jnp.concatenate(pulls, 1)

    for k in range(KERNELS):
        q = (pull * fields[k]).astype(BF)
        x = _dot(tx_ref[...], q).astype(BF)
        for t in range(2):
            at = t * 128
            xs[t, k] = jnp.concatenate([x[:32, at : at + 128], x[32:, at : at + 128]], 1)

    d = _dot(xs[...].reshape(2 * KERNELS * FREQ, 256), tv_ref[...])
    d = d.reshape(2, KERNELS, FREQ, 128)
    parts = []
    for t in range(2):
        s = jnp.sum(kk * d[t], 0)
        s = s + pltpu.roll(s, 64, 1)
        parts.append(jnp.where(occ_ref[2 * band + t, col] > 0, s, 0.0))
    out_ref[...] = jnp.where(low, parts[0], parts[1])


def _backward_kernel(
    c_ref, a_ref, b_ref, mask_ref, bwd_ref, mid_ref, left_ref, right_ref, out_ref, du
):
    @pl.when(pl.program_id(0) == 0)
    def _():
        col = lax.axis_index("img")
        odd = lax.rem(col, 2) == 1
        a = a_ref[...]
        b = jnp.where((col > 0) & (col < 31), b_ref[...], 0.0)
        left = jnp.where(odd, a, b)
        right = jnp.where(odd, b, a)
        low = _low_lanes((FREQ, 128))

        def stacked(val):
            out = []
            for r, (row, first) in enumerate(((32, True), (32, False), (0, True), (0, False))):
                x = val[row : row + 32]
                other = pltpu.roll(x, 64, 1)
                dup = jnp.where(low, x, other) if first else jnp.where(low, other, x)
                hi, lo = _split(dup)
                out.append(jnp.where(low, hi.astype(F32), lo.astype(F32)).astype(BF))
            return jnp.concatenate(out, 0)

        mid = _dot(stacked(c_ref[...]), mid_ref[...])
        lo = _dot(stacked(left), left_ref[...])
        hi = _dot(stacked(right), right_ref[...])
        for part in range(2):
            m = mid[:, part * 512 : part * 512 + 512]
            m = jnp.concatenate(
                [m[:, :128] + lo[:, part * 128 : part * 128 + 128], m[:, 128:384],
                 m[:, 384:] + hi[:, part * 128 : part * 128 + 128]], 1
            ).astype(BF)
            du[part * 64 : part * 64 + 64, :] = m[:64]
            du[128 + part * 64 : 128 + part * 64 + 64, :] = m[64:]

    values = mask_ref[...].astype(F32)
    penalty = GAMMA * 4.0 * values * (values * values - 1.0)
    out_ref[...] = _dot(bwd_ref[...], du[...]) + penalty


def _permute(value, target):
    bands, cols = lax.axis_size("own"), lax.axis_size("img")
    pairs = []
    for a in range(bands):
        for b in range(cols):
            c, d = target(a, b)
            pairs.append((a * cols + b, c * cols + d))
    return lax.ppermute(value, ("own", "img"), pairs)


def _swap_even(i, n):
    return i ^ 1


def _swap_odd(i, n):
    j = ((i + 1) ^ 1) - 1
    return j if 0 <= j < n else i


def _img_even(a, b):
    return a, _swap_even(b, 32)


def _img_odd(a, b):
    return a, _swap_odd(b, 32)


def _own_even(a, b):
    return _swap_even(a, 4), b


def _own_odd(a, b):
    return _swap_odd(a, 4), b


def on_device(mask_field, target_field, occupancy, kernels, weights):
    t = {name: jnp.asarray(value) for name, value in TABLES.items()}
    band, col = lax.axis_index("own"), lax.axis_index("img")
    vmem = pl.BlockSpec(memory_space=pltpu.VMEM)
    small = jax.ShapeDtypeStruct((64, 128), F32)

    own, send_a, send_b = pl.pallas_call(
        _forward_kernel,
        out_shape=[small] * 3,
        in_specs=[vmem] * 5,
        out_specs=[vmem] * 3,
        scratch_shapes=[pltpu.VMEM((256, 512), BF)],
        name="forward",
    )(mask_field, t["fwd"], t["f_mid"], t["f_left"], t["f_right"])

    wide = jnp.sqrt(weights)[:, None, None] * kernels
    kk = jnp.concatenate([wide[0], wide[0], wide[1], wide[1]], -1)

    got_a = _permute(send_a, _img_even)
    got_b = _permute(send_b, _img_odd)
    x1 = own + got_a + jnp.where((col > 0) & (col < 31), got_b, 0.0)
    even = lax.rem(band, 2) == 0
    ua = _permute(jnp.where(even, x1[32:], x1[:32]), _own_even)
    ub = _permute(jnp.where(even, x1[:32], x1[32:]), _own_odd)

    grads = pl.pallas_call(
        _image_kernel,
        out_shape=jax.ShapeDtypeStruct((FREQ, 128), F32),
        in_specs=[vmem] * 5 + [pl.BlockSpec(memory_space=pltpu.SMEM)] + [vmem] * 8,
        out_specs=vmem,
        scratch_shapes=[
            pltpu.VMEM((2, KERNELS, FREQ, 256), BF),
            pltpu.VMEM((2, KERNELS, FREQ, 256), BF),
            pltpu.VMEM((KERNELS, GRID, 256), F32),
            pltpu.VMEM((2, KERNELS, FREQ, 256), BF),
            pltpu.VMEM((TILE, 128), BF),
        ],
        name="image",
    )(
        x1, ua, ub, kk, target_field, occupancy,
        t["tp"], t["te"], t["tx"], t["tv"], t["tz"], t["tw"], t["ty"], t["tg"],
    )

    da = _permute(grads, _own_even)
    db = _permute(grads, _own_odd)
    inner = (band == 1) | (band == 2)
    db = jnp.where(inner, db, 0.0)
    above = jnp.where(even, db, da)
    below = jnp.where(even, da, db)
    center = jnp.concatenate([grads, jnp.concatenate([above[:, 64:], below[:, :64]], 1)], 0)
    side_a = _permute(center, _img_even)
    side_b = _permute(center, _img_odd)

    rows = 256
    whole = lambda shape: pl.BlockSpec(shape, lambda i: (0, 0))
    return pl.pallas_call(
        _backward_kernel,
        grid=(2 * TILE // rows,),
        out_shape=jax.ShapeDtypeStruct((2 * TILE, TILE), F32),
        in_specs=[whole((64, 128))] * 3
        + [
            pl.BlockSpec((rows, TILE), lambda i: (i, 0)),
            pl.BlockSpec((rows, 256), lambda i: (i, 0)),
            whole((128, 1024)),
            whole((128, 256)),
            whole((128, 256)),
        ],
        out_specs=pl.BlockSpec((rows, TILE), lambda i: (i, 0)),
        scratch_shapes=[pltpu.VMEM((256, TILE), BF)],
        name="backward",
    )(center, side_a, side_b, mask_field, t["bwd"], t["b_mid"], t["b_left"], t["b_right"])


def solution(mesh):
    return jax.shard_map(
        on_device,
        mesh=mesh,
        in_specs=(P("own", "img"), P("own", "img"), P(), P(), P()),
        out_specs=P("own", "img"),
        check_vma=False,
    )
```

```python
import jax
import jax.numpy as jnp
import numpy as np
from jax import lax
from jax.experimental import pallas as pl
from jax.experimental.pallas import tpu as pltpu
from jax.sharding import PartitionSpec as P

TILE = 512
AMBIT = 64
FREQ = 32
KERNELS = 24
PAD = 640
GRID = 64

STEEP = 2.0
THRESHOLD = 1.5
GAMMA = 0.25

BF = jnp.bfloat16
F32 = jnp.float32


def _bf(x):
    return np.asarray(x, np.float32).astype(BF)


def _hi_lo(x):
    hi = _bf(x)
    return hi, _bf(np.asarray(x, np.float64) - hi.astype(np.float64))


def _build_tables():
    f = np.arange(FREQ) - FREQ // 2
    ang = 2 * np.pi * ((f[:, None] * np.arange(PAD)[None]) % PAD) / PAD
    c = _bf(np.cos(ang) / np.sqrt(PAD)).astype(np.float64)
    s = _bf(-np.sin(ang) / np.sqrt(PAD)).astype(np.float64)

    height, width = 2 * TILE, TILE

    def rows_of(table, first, lo, hi):
        out = np.zeros((FREQ, hi - lo))
        y = np.arange(lo, hi) + first
        ok = (y >= 0) & (y < PAD)
        out[:, ok] = table[:, y[ok]]
        return out

    own_rows = [
        np.concatenate([rows_of(tb, first, 0, height), rows_of(tb, first, -AMBIT, 0), rows_of(tb, first, height, height + AMBIT)], 1)
        for first in (AMBIT, AMBIT - TILE)
        for tb in (c, s)
    ]
    fwd = np.concatenate(own_rows, 0)
    first = {0: AMBIT + TILE, 1: AMBIT, 2: AMBIT - TILE, 3: AMBIT - 2 * TILE}
    bwd = np.concatenate(
        [rows_of(tb, first[r], 0, height) for pair in ((0, 3), (1, 2)) for tb in (c, s) for r in pair], 0
    )

    def cols_of(table, shift, lo, hi):
        out = np.zeros((FREQ, hi - lo))
        x = np.arange(lo, hi) + shift
        ok = (x >= 0) & (x < PAD)
        out[:, ok] = table[:, x[ok]]
        return out

    t = {"fwd": _bf(fwd[:, :height]), "fwd_ambit": _bf(fwd[:, height:]), "bwd": _bf(bwd.T)}
    ranges = {"mid": (AMBIT, 0, width), "left": (AMBIT + TILE, 0, 128), "right": (AMBIT - TILE, width - 128, width)}
    for name, (shift, lo, hi) in ranges.items():
        cc, ss = cols_of(c, shift, lo, hi), cols_of(s, shift, lo, hi)
        re = np.concatenate([cc.T, ss.T], 1)
        im = np.concatenate([-ss.T, cc.T], 1)
        both = np.concatenate([re, im], 0)
        t["f_" + name] = _bf(np.concatenate([both, both], 1))
        dre, dim = np.concatenate([cc, ss], 0), np.concatenate([-ss, cc], 0)
        t["b_" + name] = _bf(np.concatenate([np.concatenate([dre, dre], 0), np.concatenate([dim, dim], 0)], 1))

    grid = np.arange(GRID) * (PAD // GRID)
    hang = 2 * np.pi * ((grid[:, None] * f[None]) % PAD) / PAD
    hc, hs = np.cos(hang) / np.sqrt(FREQ), np.sin(hang) / np.sqrt(FREQ)
    tp = np.concatenate(
        [
            np.concatenate([hc.T, hs.T, -hs.T, hc.T], 1),
            np.concatenate([-hs.T, hc.T, -hc.T, -hs.T], 1),
        ],
        0,
    )
    hi, lo = _hi_lo(tp)
    t["tp"] = np.concatenate([hi, hi, hi, hi, lo, lo], 0)
    hi, lo = _hi_lo(np.concatenate([hc, hs], 1))
    t["te"] = np.concatenate([hi, hi, lo], 1)
    t["tx"] = hi.T.copy()
    v1 = np.block([[hc, -hs], [hs, hc]])
    v2 = np.block([[-hs, -hc], [hc, -hs]])
    v = np.concatenate([v1, v2], 0)
    t["tv"] = _bf(np.concatenate([v, v[:, FREQ:], -v[:, :FREQ]], 1))

    n = np.arange(1 - FREQ, FREQ)
    y = np.arange(TILE) + AMBIT
    w = np.cos(2 * np.pi * ((y[:, None, None] - grid[None, :, None]) * n[None, None, :] % PAD) / PAD).sum(-1) / GRID
    hi, lo = _hi_lo(w)
    t["tz"] = np.concatenate([hi.T, hi.T, hi.T, hi.T, lo.T, lo.T], 0)
    t["tw"] = np.concatenate([hi, hi, lo], 1)
    t["ty"] = np.concatenate([hi, hi, lo, lo], 1)
    t["tg"] = np.concatenate([hi.T, lo.T], 0)
    return t


TABLES = _build_tables()


def _dot(a, b):
    return jnp.dot(a, b, preferred_element_type=F32)


def _split(x):
    hi = x.astype(BF)
    return hi, (x - hi.astype(F32)).astype(BF)


def _low_lanes(shape):
    return lax.broadcasted_iota(jnp.int32, shape, len(shape) - 1) < 64


def _forward_kernel(
    mask_ref, ha_ref, hb_ref, fwd_ref, ambit_ref, mid_ref, left_ref, right_ref, own_ref, a_ref, b_ref, acc
):
    band = lax.axis_index("own")
    even = lax.rem(band, 2) == 0
    inner = (band == 1) | (band == 2)
    odd = lax.rem(lax.axis_index("img"), 2) == 1
    ha = ha_ref[...].astype(F32)
    hb = jnp.where(inner, hb_ref[...].astype(F32), 0.0)
    ambit = jnp.concatenate([jnp.where(even, hb, ha), jnp.where(even, ha, hb)], 0).astype(BF)
    acc[...] = (_dot(fwd_ref[...], mask_ref[...]) + _dot(ambit_ref[...], ambit)).astype(BF)

    def project(lo, hi, table):
        lhs = jnp.concatenate(
            [
                jnp.concatenate([acc[0:32, lo:hi], acc[32:64, lo:hi]], 1),
                jnp.concatenate([acc[64:96, lo:hi], acc[96:128, lo:hi]], 1),
            ],
            0,
        )
        out = _dot(lhs, table[...])
        return jnp.where(_low_lanes((FREQ, 128)), out[:FREQ], out[FREQ:])

    own_ref[...] = project(0, 512, mid_ref)
    left = project(0, 128, left_ref)
    right = project(384, 512, right_ref)
    a_ref[...] = jnp.where(odd, left, right)
    b_ref[...] = jnp.where(odd, right, left)


def _image_kernel(
    x_ref, xa_ref, xb_ref, kk_ref, target_ref, occ_ref,
    tp_ref, te_ref, tx_ref, tv_ref, tz_ref, tw_ref, ty_ref, tg_ref,
    out_ref, p_hi, p_lo, fields, xs, yb,
):
    band, col = lax.axis_index("own"), lax.axis_index("img")
    m = x_ref[...] + xa_ref[...] + jnp.where((col > 0) & (col < 31), xb_ref[...], 0.0)
    turned = pltpu.roll(m, 64, 1)
    low = _low_lanes((FREQ, 128))
    lane = lax.broadcasted_iota(jnp.int32, (FREQ, 128), 1)

    kk = kk_ref[...]
    for t in range(2):
        dup = jnp.where(low, m, turned) if t == 0 else jnp.where(low, turned, m)
        swapped = pltpu.roll(dup, 32, 1)
        swapped = jnp.where(lane < 96, -swapped, swapped)
        m4 = jnp.where(low, dup, swapped)
        prod = kk * m4[None]
        hi, lo = _split(prod.reshape(KERNELS * FREQ, 128))
        half = _dot(jnp.concatenate([hi, lo, hi], 1), tp_ref[...])
        hi, lo = _split(half)
        p_hi[t] = hi.reshape(KERNELS, FREQ, 256)
        p_lo[t] = lo.reshape(KERNELS, FREQ, 256)

    total = jnp.zeros((GRID, 256), F32)
    for k in range(KERNELS):
        def halves(ref):
            return jnp.concatenate(
                [
                    jnp.concatenate([ref[0, k, :, :128], ref[1, k, :, :128]], 1),
                    jnp.concatenate([ref[0, k, :, 128:], ref[1, k, :, 128:]], 1),
                ],
                0,
            )
        hi = halves(p_hi)
        e = _dot(te_ref[...], jnp.concatenate([hi, halves(p_lo), hi], 0))
        fields[k] = e
        total = total + e * e

    hi, lo = _split(jnp.concatenate([total[:, :128], total[:, 128:]], 0))
    z = _dot(jnp.concatenate([hi, lo, hi], 1), tz_ref[...])
    pulls = []
    rows = 128
    for t in range(2):
        hi, lo = _split(z[t * GRID : (t + 1) * GRID])
        stack = jnp.concatenate([hi, lo, hi], 0)
        for c in range(TILE // rows):
            at = c * rows
            intensity = _dot(tw_ref[at : at + rows], stack)
            th = jnp.tanh((0.5 * STEEP) * (intensity - THRESHOLD))
            wanted = target_ref[t * TILE + at : t * TILE + at + rows, :].astype(F32)
            sens = (0.5 * STEEP) * (0.5 + 0.5 * th - wanted) * (1.0 - th * th)
            y = _dot(sens.astype(BF), ty_ref[...])
            yb[at : at + rows, :] = (y[:, :128] + y[:, 128:]).astype(BF)
        g = _dot(tg_ref[...], yb[...])
        pulls.append(2.0 * (g[:GRID] + g[GRID:]))
    pull = jnp.concatenate(pulls, 1)

    for k in range(KERNELS):
        q = (pull * fields[k]).astype(BF)
        x = _dot(tx_ref[...], q).astype(BF)
        for t in range(2):
            at = t * 128
            xs[t, k] = jnp.concatenate([x[:32, at : at + 128], x[32:, at : at + 128]], 1)

    d = _dot(xs[...].reshape(2 * KERNELS * FREQ, 256), tv_ref[...])
    d = d.reshape(2, KERNELS, FREQ, 128)
    parts = []
    for t in range(2):
        s = jnp.sum(kk * d[t], 0)
        s = s + pltpu.roll(s, 64, 1)
        parts.append(jnp.where(occ_ref[2 * band + t, col] > 0, s, 0.0))
    out_ref[...] = jnp.where(low, parts[0], parts[1])


def _glue_kernel(g_ref, da_ref, db_ref, out_ref):
    band = lax.axis_index("own")
    even = lax.rem(band, 2) == 0
    da = da_ref[...]
    db = jnp.where((band == 1) | (band == 2), db_ref[...], 0.0)
    above = jnp.where(even, db, da)
    below = jnp.where(even, da, db)
    out_ref[:FREQ] = g_ref[...]
    out_ref[FREQ:] = pltpu.roll(jnp.where(_low_lanes((FREQ, 128)), below, above), 64, 1)


def _stacked(val):
    low = _low_lanes((FREQ, 128))
    out = []
    for r, (row, first) in enumerate(((32, True), (32, False), (0, True), (0, False))):
        x = val[row : row + 32]
        other = pltpu.roll(x, 64, 1)
        dup = jnp.where(low, x, other) if first else jnp.where(low, other, x)
        hi, lo = _split(dup)
        out.append(jnp.where(low, hi.astype(F32), lo.astype(F32)).astype(BF))
    return jnp.concatenate(out, 0)


def _penalty(values):
    values = values.astype(F32)
    return GAMMA * 4.0 * values * (values * values - 1.0)


def _store_du(du, part, lanes, m):
    m = m.astype(BF)
    du[part * 64 : part * 64 + 64, lanes] = m[:64]
    du[128 + part * 64 : 128 + part * 64 + 64, lanes] = m[64:]


def _middle_kernel(c_ref, mask_ref, bwd_ref, mid_ref, out_ref, du):
    @pl.when(pl.program_id(0) == 0)
    def _():
        mid = _dot(_stacked(c_ref[...]), mid_ref[...])
        for part in range(2):
            _store_du(du, part, slice(0, 256), mid[:, part * 256 : part * 256 + 256])

    out_ref[...] = _dot(bwd_ref[...], du[...]) + _penalty(mask_ref[...])


def _sides_kernel(
    done_ref, c_ref, a_ref, b_ref, mask_ref, bwd_ref, mid_ref, left_ref, right_ref, out_ref, du
):
    @pl.when((pl.program_id(0) == 0) & (pl.program_id(1) == 0))
    def _():
        col = lax.axis_index("img")
        odd = lax.rem(col, 2) == 1
        a = a_ref[...]
        b = jnp.where((col > 0) & (col < 31), b_ref[...], 0.0)
        mid = _dot(_stacked(c_ref[...]), mid_ref[...])
        left = _dot(_stacked(jnp.where(odd, a, b)), left_ref[...])
        right = _dot(_stacked(jnp.where(odd, b, a)), right_ref[...])
        for part in range(2):
            at = part * 256
            _store_du(du.at[0], part, slice(0, 128), mid[:, at : at + 128] + left[:, part * 128 : part * 128 + 128])
            _store_du(du.at[1], part, slice(0, 128), mid[:, at + 128 : at + 256] + right[:, part * 128 : part * 128 + 128])

    out_ref[...] = _dot(bwd_ref[...], du[pl.program_id(1)]) + _penalty(mask_ref[...])


def _permute(value, target):
    bands, cols = lax.axis_size("own"), lax.axis_size("img")
    pairs = []
    for a in range(bands):
        for b in range(cols):
            c, d = target(a, b)
            pairs.append((a * cols + b, c * cols + d))
    return lax.ppermute(value, ("own", "img"), pairs)


def _img_even(a, b):
    return a, b ^ 1


def _img_odd(a, b):
    c = ((b + 1) ^ 1) - 1
    return (a, c) if 0 <= c < 32 else (a ^ 1, b)


def _own_even(a, b):
    return a ^ 1, b


def _own_odd(a, b):
    c = ((a + 1) ^ 1) - 1
    return (c, b) if 0 <= c < 4 else (a, b ^ 1)


def on_device(mask_field, target_field, occupancy, kernels, weights):
    t = {name: jnp.asarray(value) for name, value in TABLES.items()}
    vmem = pl.BlockSpec(memory_space=pltpu.VMEM)
    small = jax.ShapeDtypeStruct((FREQ, 128), F32)
    limit = lambda mib: pltpu.CompilerParams(vmem_limit_bytes=mib << 20)

    even = lax.rem(lax.axis_index("own"), 2) == 0
    top, bottom = mask_field[:AMBIT], mask_field[2 * TILE - AMBIT :]
    halo_a = _permute(jnp.where(even, bottom, top), _own_even)
    halo_b = _permute(jnp.where(even, top, bottom), _own_odd)

    own, send_a, send_b = pl.pallas_call(
        _forward_kernel,
        out_shape=[small] * 3,
        in_specs=[vmem] * 8,
        out_specs=[vmem] * 3,
        scratch_shapes=[pltpu.VMEM((128, 512), BF)],
        compiler_params=limit(8),
        name="forward",
    )(mask_field, halo_a, halo_b, t["fwd"], t["fwd_ambit"], t["f_mid"], t["f_left"], t["f_right"])

    wide = jnp.sqrt(weights)[:, None, None] * kernels
    kk = jnp.concatenate([wide[0], wide[0], wide[1], wide[1]], -1)

    got_a = _permute(send_a, _img_even)
    got_b = _permute(send_b, _img_odd)

    grads = pl.pallas_call(
        _image_kernel,
        out_shape=small,
        in_specs=[vmem] * 5 + [pl.BlockSpec(memory_space=pltpu.SMEM)] + [vmem] * 8,
        out_specs=vmem,
        scratch_shapes=[
            pltpu.VMEM((2, KERNELS, FREQ, 256), BF),
            pltpu.VMEM((2, KERNELS, FREQ, 256), BF),
            pltpu.VMEM((KERNELS, GRID, 256), F32),
            pltpu.VMEM((2, KERNELS, FREQ, 256), BF),
            pltpu.VMEM((TILE, 128), BF),
        ],
        compiler_params=limit(24),
        name="image",
    )(
        own, got_a, got_b, kk, target_field, occupancy,
        t["tp"], t["te"], t["tx"], t["tv"], t["tz"], t["tw"], t["ty"], t["tg"],
    )

    da = _permute(grads, _own_even)
    db = _permute(grads, _own_odd)
    center = pl.pallas_call(
        _glue_kernel,
        out_shape=jax.ShapeDtypeStruct((2 * FREQ, 128), F32),
        in_specs=[vmem] * 3,
        out_specs=vmem,
        compiler_params=limit(2),
        name="glue",
    )(grads, da, db)
    side_a = _permute(center, _img_even)
    side_b = _permute(center, _img_odd)

    rows = 256
    result = jax.ShapeDtypeStruct((2 * TILE, TILE), F32)
    whole = lambda *shape: pl.BlockSpec(shape, lambda *i: (0, 0))
    b_mid = t["b_mid"]
    cut = lambda lo, hi: [b_mid[:, lo:hi], b_mid[:, TILE + lo : TILE + hi]]
    b_in = jnp.concatenate(cut(128, 384), 1)
    b_out = jnp.concatenate([x for p in (0, TILE) for x in (b_mid[:, p : p + 128], b_mid[:, p + 384 : p + 512])], 1)
    inside = pl.BlockSpec((pl.Element(rows), pl.Element(256)), lambda i: (i * rows, 128))
    middle = pl.pallas_call(
        _middle_kernel,
        grid=(2 * TILE // rows,),
        out_shape=result,
        in_specs=[
            whole(2 * FREQ, 128),
            inside,
            pl.BlockSpec((rows, 256), lambda i: (i, 0)),
            whole(128, 512),
        ],
        out_specs=inside,
        scratch_shapes=[pltpu.VMEM((256, 256), BF)],
        compiler_params=limit(8),
        name="middle",
    )(center, mask_field, t["bwd"], b_in)
    edge = pl.BlockSpec((rows, 128), lambda i, j: (i, 3 * j))
    return pl.pallas_call(
        _sides_kernel,
        grid=(2 * TILE // rows, 2),
        out_shape=result,
        in_specs=[pl.BlockSpec(memory_space=pl.ANY)]
        + [whole(2 * FREQ, 128)] * 3
        + [
            edge,
            pl.BlockSpec((rows, 256), lambda i, j: (i, 0)),
            whole(128, 512),
            whole(128, 256),
            whole(128, 256),
        ],
        out_specs=edge,
        scratch_shapes=[pltpu.VMEM((2, 256, 128), BF)],
        input_output_aliases={0: 0},
        compiler_params=limit(8),
        name="sides",
    )(middle, center, side_a, side_b, mask_field, t["bwd"], b_out, t["b_left"], t["b_right"])


def solution(mesh):
    return jax.shard_map(
        on_device,
        mesh=mesh,
        in_specs=(P("own", "img"), P("own", "img"), P(), P(), P()),
        out_specs=P("own", "img"),
        check_vma=False,
    )
```

```python
import jax
import jax.numpy as jnp
import numpy as np
from jax import lax
from jax.experimental import pallas as pl
from jax.experimental.pallas import tpu as pltpu
from jax.sharding import PartitionSpec as P

TILE = 512
AMBIT = 64
FREQ = 32
KERNELS = 24
PAD = 640
GRID = 64

STEEP = 2.0
THRESHOLD = 1.5
GAMMA = 0.25

BF = jnp.bfloat16
F32 = jnp.float32


def _bf(x):
    return np.asarray(x, np.float32).astype(BF)


def _hi_lo(x):
    hi = _bf(x)
    return hi, _bf(np.asarray(x, np.float64) - hi.astype(np.float64))


def _build_tables():
    f = np.arange(FREQ) - FREQ // 2
    ang = 2 * np.pi * ((f[:, None] * np.arange(PAD)[None]) % PAD) / PAD
    c = _bf(np.cos(ang) / np.sqrt(PAD)).astype(np.float64)
    s = _bf(-np.sin(ang) / np.sqrt(PAD)).astype(np.float64)

    height, width = 2 * TILE, TILE

    def rows_of(table, first, lo, hi):
        out = np.zeros((FREQ, hi - lo))
        y = np.arange(lo, hi) + first
        ok = (y >= 0) & (y < PAD)
        out[:, ok] = table[:, y[ok]]
        return out

    own_rows = [
        np.concatenate([rows_of(tb, first, 0, height), rows_of(tb, first, -AMBIT, 0), rows_of(tb, first, height, height + AMBIT)], 1)
        for first in (AMBIT, AMBIT - TILE)
        for tb in (c, s)
    ]
    fwd = np.concatenate(own_rows, 0)
    first = {0: AMBIT + TILE, 1: AMBIT, 2: AMBIT - TILE, 3: AMBIT - 2 * TILE}
    bwd = np.concatenate([rows_of(tb, first[r], 0, height) for tb in (c, s) for r in (1, 2)], 0)
    far = np.concatenate(
        [
            np.concatenate([rows_of(tb, first[0], 0, AMBIT).T for tb in (c, s)], 1),
            np.concatenate([rows_of(tb, first[3], height - AMBIT, height).T for tb in (c, s)], 1),
        ],
        0,
    )

    def cols_of(table, shift, lo, hi):
        out = np.zeros((FREQ, hi - lo))
        x = np.arange(lo, hi) + shift
        ok = (x >= 0) & (x < PAD)
        out[:, ok] = table[:, x[ok]]
        return out

    t = {"fwd": _bf(fwd[:, :height]), "fwd_ambit": _bf(fwd[:, height:]), "bwd": _bf(bwd.T), "far": _bf(far)}
    ranges = {"mid": (AMBIT, 0, width), "left": (AMBIT + TILE, 0, 128), "right": (AMBIT - TILE, width - 128, width)}
    for name, (shift, lo, hi) in ranges.items():
        cc, ss = cols_of(c, shift, lo, hi), cols_of(s, shift, lo, hi)
        re = np.concatenate([cc.T, ss.T], 1)
        im = np.concatenate([-ss.T, cc.T], 1)
        both = np.concatenate([re, im], 0)
        t["f_" + name] = _bf(np.concatenate([both, both], 1))
        dre, dim = np.concatenate([cc, ss], 0), np.concatenate([-ss, cc], 0)
        t["b_" + name] = _bf(np.concatenate([np.concatenate([dre, dre], 0), np.concatenate([dim, dim], 0)], 1))

    side = np.concatenate([t.pop("b_left"), t.pop("b_right")], 0)
    t["b_side"] = side

    grid = np.arange(GRID) * (PAD // GRID)
    hang = 2 * np.pi * ((grid[:, None] * f[None]) % PAD) / PAD
    hc, hs = np.cos(hang) / np.sqrt(FREQ), np.sin(hang) / np.sqrt(FREQ)
    tp = np.concatenate(
        [
            np.concatenate([hc.T, hs.T, -hs.T, hc.T], 1),
            np.concatenate([-hs.T, hc.T, -hc.T, -hs.T], 1),
        ],
        0,
    )
    hi, lo = _hi_lo(tp)
    t["tp"] = np.concatenate([hi, hi, lo, lo], 0)
    hi, lo = _hi_lo(np.concatenate([hc, hs], 1))
    t["te"] = np.concatenate([hi, lo], 1)
    t["tx"] = hi.T.copy()
    v1 = np.block([[hc, -hs], [hs, hc]])
    v2 = np.block([[-hs, -hc], [hc, -hs]])
    v = np.concatenate([v1, v2], 0)
    t["tv"] = _bf(np.concatenate([v, v[:, FREQ:], -v[:, :FREQ]], 1))

    n = np.arange(1 - FREQ, FREQ)
    y = np.arange(TILE) + AMBIT
    w = np.cos(2 * np.pi * ((y[:, None, None] - grid[None, :, None]) * n[None, None, :] % PAD) / PAD).sum(-1) / GRID
    hi, lo = _hi_lo(w)
    t["tz"] = np.concatenate([hi.T, hi.T, hi.T, hi.T, lo.T, lo.T], 0)
    t["tw"] = np.concatenate([hi, hi, lo, np.ones((TILE, 1), BF), np.zeros((TILE, 15), BF)], 1)
    t["ty"] = np.concatenate([hi, hi, lo, lo], 1)
    t["tg"] = np.concatenate([hi.T, lo.T], 0)
    return t


TABLES = _build_tables()


def _dot(a, b):
    return jnp.dot(a, b, preferred_element_type=F32)


def _split(x):
    hi = x.astype(BF)
    return hi, (x - hi.astype(F32)).astype(BF)


def _low_lanes(shape):
    return lax.broadcasted_iota(jnp.int32, shape, len(shape) - 1) < 64


def _forward_kernel(
    mask_ref, ha_ref, hb_ref, fwd_ref, ambit_ref, mid_ref, left_ref, right_ref, own_ref, a_ref, b_ref, acc
):
    band = lax.axis_index("own")
    even = lax.rem(band, 2) == 0
    inner = (band == 1) | (band == 2)
    odd = lax.rem(lax.axis_index("img"), 2) == 1
    ha = ha_ref[...].astype(F32)
    hb = jnp.where(inner, hb_ref[...].astype(F32), 0.0)
    ambit = jnp.concatenate([jnp.where(even, hb, ha), jnp.where(even, ha, hb)], 0).astype(BF)
    acc[...] = (_dot(fwd_ref[...], mask_ref[...]) + _dot(ambit_ref[...], ambit)).astype(BF)

    def project(lo, hi, table):
        lhs = jnp.concatenate(
            [
                jnp.concatenate([acc[0:32, lo:hi], acc[32:64, lo:hi]], 1),
                jnp.concatenate([acc[64:96, lo:hi], acc[96:128, lo:hi]], 1),
            ],
            0,
        )
        out = _dot(lhs, table[...])
        return jnp.where(_low_lanes((FREQ, 128)), out[:FREQ], out[FREQ:])

    own_ref[...] = project(0, 512, mid_ref)
    left = project(0, 128, left_ref)
    right = project(384, 512, right_ref)
    a_ref[...] = jnp.where(odd, left, right)
    b_ref[...] = jnp.where(odd, right, left)


def _image_kernel(
    x_ref, xa_ref, xb_ref, kk_ref, target_ref, occ_ref,
    tp_ref, te_ref, tx_ref, tv_ref, tz_ref, tw_ref, ty_ref, tg_ref,
    out_ref, p_hi, fields, xs, yb,
):
    band, col = lax.axis_index("own"), lax.axis_index("img")
    m = x_ref[...] + xa_ref[...] + jnp.where((col > 0) & (col < 31), xb_ref[...], 0.0)
    turned = pltpu.roll(m, 64, 1)
    low = _low_lanes((FREQ, 128))
    lane = lax.broadcasted_iota(jnp.int32, (FREQ, 128), 1)

    kk = kk_ref[...]
    for t in range(2):
        dup = jnp.where(low, m, turned) if t == 0 else jnp.where(low, turned, m)
        swapped = pltpu.roll(dup, 32, 1)
        swapped = jnp.where(lane < 96, -swapped, swapped)
        m4 = jnp.where(low, dup, swapped)
        prod = kk * m4[None]
        prod = prod.reshape(KERNELS * FREQ, 128).astype(BF)
        half = _dot(jnp.concatenate([prod, prod], 1), tp_ref[...])
        p_hi[t] = half.astype(BF).reshape(KERNELS, FREQ, 256)

    total = jnp.zeros((GRID, 256), F32)
    for k in range(KERNELS):
        def halves(ref):
            return jnp.concatenate(
                [
                    jnp.concatenate([ref[0, k, :, :128], ref[1, k, :, :128]], 1),
                    jnp.concatenate([ref[0, k, :, 128:], ref[1, k, :, 128:]], 1),
                ],
                0,
            )
        hi = halves(p_hi)
        e = _dot(te_ref[...], jnp.concatenate([hi, hi], 0))
        fields[k] = e
        total = total + e * e

    hi, lo = _split(jnp.concatenate([total[:, :128], total[:, 128:]], 0))
    z = _dot(jnp.concatenate([hi, lo, hi], 1), tz_ref[...])
    pulls = []
    rows = 128
    for t in range(2):
        hi, lo = _split(z[t * GRID : (t + 1) * GRID])
        stack = jnp.concatenate([hi, lo, hi, jnp.full((16, TILE), -THRESHOLD, BF)], 0)
        for c in range(TILE // rows):
            at = c * rows
            over = _dot(tw_ref[at : at + rows], stack)
            th = jnp.tanh((0.5 * STEEP) * over)
            sens = ((th + 1.0) - 2.0 * target_ref[t * TILE + at : t * TILE + at + rows, :].astype(F32)) * (1.0 - th * th)
            y = _dot(sens.astype(BF), ty_ref[...])
            yb[at : at + rows, :] = (y[:, :128] + y[:, 128:]).astype(BF)
        g = _dot(tg_ref[...], yb[...])
        pulls.append((0.5 * STEEP) * (g[:GRID] + g[GRID:]))
    pull = jnp.concatenate(pulls, 1)

    for k in range(KERNELS):
        q = (pull * fields[k]).astype(BF)
        x = _dot(tx_ref[...], q).astype(BF)
        for t in range(2):
            at = t * 128
            xs[t, k] = jnp.concatenate([x[:32, at : at + 128], x[32:, at : at + 128]], 1)

    d = _dot(xs[...].reshape(2 * KERNELS * FREQ, 256), tv_ref[...])
    d = d.reshape(2, KERNELS, FREQ, 128)
    parts = []
    for t in range(2):
        s = jnp.sum(kk * d[t], 0)
        s = s + pltpu.roll(s, 64, 1)
        parts.append(jnp.where(occ_ref[2 * band + t, col] > 0, s, 0.0))
    out_ref[...] = jnp.where(low, parts[0], parts[1])


def _glue_kernel(done_ref, g_ref, sa_ref, sb_ref, ta_ref, tb_ref):
    even = lax.rem(lax.axis_index("own"), 2) == 0
    low = _low_lanes((FREQ, 128))
    own = g_ref[...]
    left, right = _by_side(sa_ref, sb_ref)
    turn = lambda x: pltpu.roll(x, 64, 1)
    first = jnp.concatenate([jnp.where(low, own, turn(left)), jnp.where(low, right, 0.0)], 0)
    second = jnp.concatenate([jnp.where(low, turn(own), left), jnp.where(low, turn(right), 0.0)], 0)
    ta_ref[...] = jnp.where(even, second, first)
    tb_ref[...] = jnp.where(even, first, second)


def _by_side(sa_ref, sb_ref):
    col = lax.axis_index("img")
    odd = lax.rem(col, 2) == 1
    a = sa_ref[...]
    b = jnp.where((col > 0) & (col < 31), sb_ref[...], 0.0)
    return jnp.where(odd, a, b), jnp.where(odd, b, a)


def _spread(val, which):
    low = _low_lanes((FREQ, 128))
    other = pltpu.roll(val, 64, 1)
    dup = jnp.where(low, val, other) if which == 0 else jnp.where(low, other, val)
    hi, lo = _split(dup)
    return jnp.where(low, hi.astype(F32), lo.astype(F32)).astype(BF)


def _stacked(val):
    return jnp.concatenate([_spread(val, 0), _spread(val, 1)], 0)


def _penalty(values):
    values = values.astype(F32)
    return GAMMA * 4.0 * values * (values * values - 1.0)


ROWS = 256
CHUNKS = tuple((i * ROWS + (AMBIT if i == 0 else 0), (i + 1) * ROWS - (AMBIT if i == 3 else 0)) for i in range(4))


def _inner_kernel(g_ref, mask_ref, bwd_ref, mid_ref, out_ref, edge_ref, rim_ref, du, staged, sem):
    mid = _dot(_stacked(g_ref[...]), mid_ref[...]).astype(BF)
    du[:64] = mid[:, :TILE]
    du[64:] = mid[:, TILE:]
    copies = []
    for i, (lo, hi) in enumerate(CHUNKS):
        rows = pl.ds(i * ROWS, ROWS)
        g = _dot(bwd_ref[rows, :], du[...]) + _penalty(mask_ref[rows, :])
        staged[rows, :] = g[:, 128:384]
        copy = pltpu.make_async_copy(
            staged.at[pl.ds(lo, hi - lo)], out_ref.at[pl.ds(lo, hi - lo), pl.ds(128, 256)], sem.at[i]
        )
        copy.start()
        copies.append(copy)
        edge_ref[rows, :128] = g[:, :128]
        edge_ref[rows, 128:] = g[:, 384:]
        if i == 0:
            rim_ref[:AMBIT] = g[:AMBIT, 128:384]
        if i == 3:
            rim_ref[AMBIT:] = g[ROWS - AMBIT :, 128:384]
    for copy in copies:
        copy.wait()


def _sides_kernel(done_ref, edge_ref, rim_ref, sa_ref, sb_ref, bwd_ref, side_ref, out_ref, part_ref, du, staged, sem):
    left, right = _by_side(sa_ref, sb_ref)
    lhs = jnp.concatenate([_stacked(left), _stacked(right)], 1)
    both = _dot(lhs, side_ref[...]).astype(BF)
    du[:64] = both[:, :128]
    du[64:] = both[:, 128:]
    low = _low_lanes((ROWS, 128))
    part_ref[:, 128:384] = rim_ref[...]
    copies = []
    for i, (lo, hi) in enumerate(CHUNKS):
        rows = pl.ds(i * ROWS, ROWS)
        g = _dot(bwd_ref[rows, :], du[...])
        for side in range(2):
            lanes = pl.ds(side * 128, 128)
            whole = edge_ref[rows, lanes] + (jnp.where(low, g, 0.0) if side == 0 else jnp.where(low, 0.0, g))
            staged[rows, lanes] = whole
            copy = pltpu.make_async_copy(
                staged.at[pl.ds(lo, hi - lo), lanes],
                out_ref.at[pl.ds(lo, hi - lo), pl.ds(side * 384, 128)],
                sem.at[2 * i + side],
            )
            copy.start()
            copies.append(copy)
            if i == 0:
                part_ref[:AMBIT, side * 384 : side * 384 + 128] = whole[:AMBIT]
            if i == 3:
                part_ref[AMBIT:, side * 384 : side * 384 + 128] = whole[ROWS - AMBIT :]
    for copy in copies:
        copy.wait()


def _rims_kernel(done_ref, part_ref, ta_ref, tb_ref, far_ref, mid_ref, side_ref, out_ref, staged, sem):
    band = lax.axis_index("own")
    even = lax.rem(band, 2) == 0
    ta = ta_ref[...]
    tb = jnp.where((band == 1) | (band == 2), tb_ref[...], 0.0)
    own, near = [], []
    for got in (jnp.where(even, tb, ta), jnp.where(even, ta, tb)):
        own.append(_spread(got[:FREQ], 0))
        near.append(jnp.concatenate([_spread(got[:FREQ], 1), _spread(got[FREQ:], 0)], 1))
    du = _dot(jnp.concatenate(own, 0), mid_ref[...])
    both = _dot(jnp.concatenate(near, 0), side_ref[...])
    low = _low_lanes((2 * FREQ, 128))
    parts = []
    for p in range(2):
        d, n = du[:, p * TILE : p * TILE + TILE], both[:, p * 128 : p * 128 + 128]
        parts.append(
            jnp.concatenate(
                [d[:, :128] + jnp.where(low, n, 0.0), d[:, 128:384], d[:, 384:] + jnp.where(low, 0.0, n)], 1
            ).astype(BF)
        )
    copies = []
    for side in range(2):
        rows = pl.ds(side * AMBIT, AMBIT)
        stack = jnp.concatenate([p[side * FREQ : side * FREQ + FREQ] for p in parts], 0)
        staged[rows, :] = part_ref[rows, :] + _dot(far_ref[rows, :], stack)
        copy = pltpu.make_async_copy(
            staged.at[rows], out_ref.at[pl.ds(side * (2 * TILE - AMBIT), AMBIT)], sem.at[side]
        )
        copy.start()
        copies.append(copy)
    for copy in copies:
        copy.wait()


def _permute(value, target):
    bands, cols = lax.axis_size("own"), lax.axis_size("img")
    pairs = []
    for a in range(bands):
        for b in range(cols):
            c, d = target(a, b)
            pairs.append((a * cols + b, c * cols + d))
    return lax.ppermute(value, ("own", "img"), pairs)


def _img_even(a, b):
    return a, b ^ 1


def _img_odd(a, b):
    c = ((b + 1) ^ 1) - 1
    return (a, c) if 0 <= c < 32 else (a ^ 1, b)


def _own_even(a, b):
    return a ^ 1, b


def _own_odd(a, b):
    c = ((a + 1) ^ 1) - 1
    return (c, b) if 0 <= c < 4 else (a, b ^ 1)


def on_device(mask_field, target_field, occupancy, kernels, weights):
    t = {name: jnp.asarray(value) for name, value in TABLES.items()}
    vmem = pl.BlockSpec(memory_space=pltpu.VMEM)
    small = jax.ShapeDtypeStruct((FREQ, 128), F32)
    limit = lambda mib: pltpu.CompilerParams(vmem_limit_bytes=mib << 20)

    hbm = pl.BlockSpec(memory_space=pltpu.MemorySpace.HBM)
    even = lax.rem(lax.axis_index("own"), 2) == 0
    top, bottom = mask_field[:AMBIT], mask_field[2 * TILE - AMBIT :]
    ambit_a = jnp.where(even, bottom, top)
    ambit_b = jnp.where(even, top, bottom)
    halo_a = _permute(ambit_a, _own_even)
    halo_b = _permute(ambit_b, _own_odd)

    smem = pl.BlockSpec(memory_space=pltpu.SMEM)
    wide = jnp.sqrt(weights)[:, None, None] * kernels
    kk = jnp.concatenate([wide[0], wide[0], wide[1], wide[1]], -1)

    own, send_a, send_b = pl.pallas_call(
        _forward_kernel,
        out_shape=[small] * 3,
        in_specs=[vmem] * 8,
        out_specs=[vmem] * 3,
        scratch_shapes=[pltpu.VMEM((128, 512), BF)],
        compiler_params=limit(8),
        name="forward",
    )(mask_field, halo_a, halo_b, t["fwd"], t["fwd_ambit"], t["f_mid"], t["f_left"], t["f_right"])

    got_a = _permute(send_a, _img_even)
    got_b = _permute(send_b, _img_odd)

    grads = pl.pallas_call(
        _image_kernel,
        out_shape=small,
        in_specs=[vmem] * 5 + [smem] + [vmem] * 8,
        out_specs=vmem,
        scratch_shapes=[
            pltpu.VMEM((2, KERNELS, FREQ, 256), BF),
            pltpu.VMEM((KERNELS, GRID, 256), F32),
            pltpu.VMEM((2, KERNELS, FREQ, 256), BF),
            pltpu.VMEM((TILE, 128), BF),
        ],
        compiler_params=limit(24),
        name="image",
    )(
        own, got_a, got_b, kk, target_field, occupancy,
        t["tp"], t["te"], t["tx"], t["tv"], t["tz"], t["tw"], t["ty"], t["tg"],
    )

    side_a = _permute(grads, _img_even)
    side_b = _permute(grads, _img_odd)

    result = jax.ShapeDtypeStruct((2 * TILE, TILE), F32)
    middle, edges, rims = pl.pallas_call(
        _inner_kernel,
        out_shape=[result, jax.ShapeDtypeStruct((2 * TILE, 256), F32), jax.ShapeDtypeStruct((2 * AMBIT, 256), F32)],
        in_specs=[vmem] * 4,
        out_specs=[hbm, vmem, vmem],
        scratch_shapes=[
            pltpu.VMEM((128, TILE), BF),
            pltpu.VMEM((2 * TILE, 256), F32),
            pltpu.SemaphoreType.DMA((4,)),
        ],
        compiler_params=limit(8),
        name="inner",
    )(grads, mask_field, t["bwd"], t["b_mid"])

    pair = jax.ShapeDtypeStruct((2 * FREQ, 128), F32)
    send_a, send_b = pl.pallas_call(
        _glue_kernel,
        out_shape=[pair] * 2,
        in_specs=[vmem] * 4,
        out_specs=[vmem] * 2,
        compiler_params=limit(2),
        name="glue",
    )(rims, grads, side_a, side_b)
    tile_a = _permute(send_a, _own_even)
    tile_b = _permute(send_b, _own_odd)

    most, part = pl.pallas_call(
        _sides_kernel,
        out_shape=[result, jax.ShapeDtypeStruct((2 * AMBIT, TILE), F32)],
        in_specs=[hbm] + [vmem] * 6,
        out_specs=[hbm, vmem],
        scratch_shapes=[
            pltpu.VMEM((128, 128), BF),
            pltpu.VMEM((2 * TILE, 256), F32),
            pltpu.SemaphoreType.DMA((8,)),
        ],
        input_output_aliases={0: 0},
        compiler_params=limit(8),
        name="sides",
    )(middle, edges, rims, side_a, side_b, t["bwd"], t["b_side"])
    return pl.pallas_call(
        _rims_kernel,
        out_shape=result,
        in_specs=[hbm] + [vmem] * 6,
        out_specs=hbm,
        scratch_shapes=[pltpu.VMEM((2 * AMBIT, TILE), F32), pltpu.SemaphoreType.DMA((2,))],
        input_output_aliases={0: 0},
        compiler_params=limit(4),
        name="rims",
    )(most, part, tile_a, tile_b, t["far"], t["b_mid"], t["b_side"])


def solution(mesh):
    return jax.shard_map(
        on_device,
        mesh=mesh,
        in_specs=(P("own", "img"), P("own", "img"), P(), P(), P()),
        out_specs=P("own", "img"),
        check_vma=False,
    )
```

```python
import jax
import jax.numpy as jnp
import numpy as np
from jax import lax
from jax.experimental import pallas as pl
from jax.experimental.pallas import tpu as pltpu
from jax.sharding import PartitionSpec as P


TILE = 512
AMBIT = 64
FREQ = 32
KERNELS = 24
PAD = 640
GRID = 64

STEEP = 2.0
THRESHOLD = 1.5
GAMMA = 0.25

BF = jnp.bfloat16
F32 = jnp.float32


def _bf(x):
    return np.asarray(x, np.float32).astype(BF)


def _hi_lo(x):
    hi = _bf(x)
    return hi, _bf(np.asarray(x, np.float64) - hi.astype(np.float64))


def _build_tables():
    f = np.arange(FREQ) - FREQ // 2
    ang = 2 * np.pi * ((f[:, None] * np.arange(PAD)[None]) % PAD) / PAD
    c = _bf(np.cos(ang) / np.sqrt(PAD)).astype(np.float64)
    s = _bf(-np.sin(ang) / np.sqrt(PAD)).astype(np.float64)

    height, width = 2 * TILE, TILE

    def rows_of(table, first, lo, hi):
        out = np.zeros((FREQ, hi - lo))
        y = np.arange(lo, hi) + first
        ok = (y >= 0) & (y < PAD)
        out[:, ok] = table[:, y[ok]]
        return out

    own_rows = [
        np.concatenate([rows_of(tb, first, 0, height), rows_of(tb, first, -AMBIT, 0), rows_of(tb, first, height, height + AMBIT)], 1)
        for first in (AMBIT, AMBIT - TILE)
        for tb in (c, s)
    ]
    fwd = np.concatenate(own_rows, 0)
    first = {0: AMBIT + TILE, 1: AMBIT, 2: AMBIT - TILE, 3: AMBIT - 2 * TILE}
    bwd = np.concatenate([rows_of(tb, first[r], 0, height) for tb in (c, s) for r in (1, 2)], 0)
    far = np.concatenate(
        [
            np.concatenate([rows_of(tb, first[0], 0, AMBIT).T for tb in (c, s)], 1),
            np.concatenate([rows_of(tb, first[3], height - AMBIT, height).T for tb in (c, s)], 1),
        ],
        0,
    )

    def cols_of(table, shift, lo, hi):
        out = np.zeros((FREQ, hi - lo))
        x = np.arange(lo, hi) + shift
        ok = (x >= 0) & (x < PAD)
        out[:, ok] = table[:, x[ok]]
        return out

    t = {"fwd": _bf(fwd[:, :height]), "fwd_ambit": _bf(fwd[:, height:]), "bwd": _bf(bwd.T), "far": _bf(far)}
    ranges = {"mid": (AMBIT, 0, width), "left": (AMBIT + TILE, 0, 128), "right": (AMBIT - TILE, width - 128, width)}
    for name, (shift, lo, hi) in ranges.items():
        cc, ss = cols_of(c, shift, lo, hi), cols_of(s, shift, lo, hi)
        re = np.concatenate([cc.T, ss.T], 1)
        im = np.concatenate([-ss.T, cc.T], 1)
        both = np.concatenate([re, im], 0)
        t["f_" + name] = _bf(np.concatenate([both, both], 1))
        dre, dim = np.concatenate([cc, ss], 0), np.concatenate([-ss, cc], 0)
        t["b_" + name] = _bf(np.concatenate([np.concatenate([dre, dre], 0), np.concatenate([dim, dim], 0)], 1))

    side = np.concatenate([t.pop("b_left"), t.pop("b_right")], 0)
    t["b_side"] = side

    grid = np.arange(GRID) * (PAD // GRID)
    hang = 2 * np.pi * ((grid[:, None] * f[None]) % PAD) / PAD
    hc, hs = np.cos(hang) / np.sqrt(FREQ), np.sin(hang) / np.sqrt(FREQ)
    tp = np.concatenate(
        [
            np.concatenate([hc.T, hs.T, -hs.T, hc.T], 1),
            np.concatenate([-hs.T, hc.T, -hc.T, -hs.T], 1),
        ],
        0,
    )
    hi, lo = _hi_lo(tp)
    t["tp"] = np.concatenate([hi, hi, lo, lo], 0)
    hi, lo = _hi_lo(np.concatenate([hc, hs], 1))
    t["te"] = np.concatenate([hi, lo], 1)
    t["tx"] = hi.T.copy()
    v1 = np.block([[hc, -hs], [hs, hc]])
    v2 = np.block([[-hs, -hc], [hc, -hs]])
    v = np.concatenate([v1, v2], 0)
    t["tv"] = _bf(np.concatenate([v, v[:, FREQ:], -v[:, :FREQ]], 1))

    n = np.arange(1 - FREQ, FREQ)
    y = np.arange(TILE) + AMBIT
    w = np.cos(2 * np.pi * ((y[:, None, None] - grid[None, :, None]) * n[None, None, :] % PAD) / PAD).sum(-1) / GRID
    hi, lo = _hi_lo(w)
    t["tz"] = np.concatenate([hi.T, hi.T, hi.T, hi.T, lo.T, lo.T], 0)
    t["tw"] = np.concatenate([hi, hi, lo, np.ones((TILE, 1), BF), np.zeros((TILE, 15), BF)], 1)
    t["ty"] = np.concatenate([hi, hi, lo, lo], 1)
    t["tg"] = np.concatenate([hi.T, lo.T], 0)
    return t


TABLES = _build_tables()


def _dot(a, b):
    return jnp.dot(a, b, preferred_element_type=F32)


def _split(x):
    hi = x.astype(BF)
    return hi, (x - hi.astype(F32)).astype(BF)


def _low_lanes(shape):
    return lax.broadcasted_iota(jnp.int32, shape, len(shape) - 1) < 64


def _forward_kernel(
    mask_ref, ha_ref, hb_ref, fwd_ref, ambit_ref, mid_ref, left_ref, right_ref, own_ref, a_ref, b_ref, acc
):
    band = lax.axis_index("own")
    even = lax.rem(band, 2) == 0
    inner = (band == 1) | (band == 2)
    odd = lax.rem(lax.axis_index("img"), 2) == 1
    ha = ha_ref[...].astype(F32)
    hb = jnp.where(inner, hb_ref[...].astype(F32), 0.0)
    ambit = jnp.concatenate([jnp.where(even, hb, ha), jnp.where(even, ha, hb)], 0).astype(BF)
    acc[...] = (_dot(fwd_ref[...], mask_ref[...]) + _dot(ambit_ref[...], ambit)).astype(BF)

    def project(lo, hi, table):
        lhs = jnp.concatenate(
            [
                jnp.concatenate([acc[0:32, lo:hi], acc[32:64, lo:hi]], 1),
                jnp.concatenate([acc[64:96, lo:hi], acc[96:128, lo:hi]], 1),
            ],
            0,
        )
        out = _dot(lhs, table[...])
        return jnp.where(_low_lanes((FREQ, 128)), out[:FREQ], out[FREQ:])

    own_ref[...] = project(0, 512, mid_ref)
    left = project(0, 128, left_ref)
    right = project(384, 512, right_ref)
    a_ref[...] = jnp.where(odd, left, right)
    b_ref[...] = jnp.where(odd, right, left)


def _image_kernel(
    x_ref, xa_ref, xb_ref, kk_ref, target_ref, occ_ref,
    tp_ref, te_ref, tx_ref, tv_ref, tz_ref, tw_ref, ty_ref, tg_ref,
    out_ref, p_hi, fields, xs, yb,
):
    band, col = lax.axis_index("own"), lax.axis_index("img")
    m = x_ref[...] + xa_ref[...] + jnp.where((col > 0) & (col < 31), xb_ref[...], 0.0)
    turned = pltpu.roll(m, 64, 1)
    low = _low_lanes((FREQ, 128))
    lane = lax.broadcasted_iota(jnp.int32, (FREQ, 128), 1)

    kk = kk_ref[...]
    for t in range(2):
        dup = jnp.where(low, m, turned) if t == 0 else jnp.where(low, turned, m)
        swapped = pltpu.roll(dup, 32, 1)
        swapped = jnp.where(lane < 96, -swapped, swapped)
        m4 = jnp.where(low, dup, swapped)
        prod = kk * m4[None]
        prod = prod.reshape(KERNELS * FREQ, 128).astype(BF)
        half = _dot(jnp.concatenate([prod, prod], 1), tp_ref[...])
        p_hi[t] = half.astype(BF).reshape(KERNELS, FREQ, 256)

    total = jnp.zeros((GRID, 256), F32)
    for k in range(KERNELS):
        def halves(ref):
            return jnp.concatenate(
                [
                    jnp.concatenate([ref[0, k, :, :128], ref[1, k, :, :128]], 1),
                    jnp.concatenate([ref[0, k, :, 128:], ref[1, k, :, 128:]], 1),
                ],
                0,
            )

        hi = halves(p_hi)
        e = _dot(te_ref[...], jnp.concatenate([hi, hi], 0))
        fields[k] = e
        total = total + e * e

    hi, lo = _split(jnp.concatenate([total[:, :128], total[:, 128:]], 0))
    z = _dot(jnp.concatenate([hi, lo, hi], 1), tz_ref[...])
    pulls = []
    rows = 128
    for t in range(2):
        hi, lo = _split(z[t * GRID : (t + 1) * GRID])
        stack = jnp.concatenate([hi, lo, hi, jnp.full((16, TILE), -THRESHOLD, BF)], 0)
        for c in range(TILE // rows):
            at = c * rows
            over = _dot(tw_ref[at : at + rows], stack)
            th = jnp.tanh((0.5 * STEEP) * over)
            sens = ((th + 1.0) - 2.0 * target_ref[t * TILE + at : t * TILE + at + rows, :].astype(F32)) * (1.0 - th * th)
            y = _dot(sens.astype(BF), ty_ref[...])
            yb[at : at + rows, :] = (y[:, :128] + y[:, 128:]).astype(BF)
        g = _dot(tg_ref[...], yb[...])
        pulls.append((0.5 * STEEP) * (g[:GRID] + g[GRID:]))
    pull = jnp.concatenate(pulls, 1)

    for k in range(KERNELS):
        q = (pull * fields[k]).astype(BF)
        x = _dot(tx_ref[...], q).astype(BF)
        for t in range(2):
            at = t * 128
            xs[t, k] = jnp.concatenate([x[:32, at : at + 128], x[32:, at : at + 128]], 1)

    d = _dot(xs[...].reshape(2 * KERNELS * FREQ, 256), tv_ref[...])
    d = d.reshape(2, KERNELS, FREQ, 128)
    parts = []
    for t in range(2):
        s = jnp.sum(kk * d[t], 0)
        s = s + pltpu.roll(s, 64, 1)
        parts.append(jnp.where(occ_ref[2 * band + t, col] > 0, s, 0.0))
    out_ref[...] = jnp.where(low, parts[0], parts[1])


def _glue_kernel(done_ref, g_ref, sa_ref, sb_ref, ta_ref, tb_ref):
    even = lax.rem(lax.axis_index("own"), 2) == 0
    low = _low_lanes((FREQ, 128))
    own = g_ref[...]
    left, right = _by_side(sa_ref, sb_ref)
    turn = lambda x: pltpu.roll(x, 64, 1)
    first = jnp.concatenate([jnp.where(low, own, turn(left)), jnp.where(low, right, 0.0)], 0)
    second = jnp.concatenate([jnp.where(low, turn(own), left), jnp.where(low, turn(right), 0.0)], 0)
    ta_ref[...] = jnp.where(even, second, first).astype(BF)
    tb_ref[...] = jnp.where(even, first, second).astype(BF)


def _by_side(sa_ref, sb_ref):
    col = lax.axis_index("img")
    odd = lax.rem(col, 2) == 1
    a = sa_ref[...]
    b = jnp.where((col > 0) & (col < 31), sb_ref[...], 0.0)
    return jnp.where(odd, a, b), jnp.where(odd, b, a)


def _spread(val, which):
    low = _low_lanes((FREQ, 128))
    other = pltpu.roll(val, 64, 1)
    dup = jnp.where(low, val, other) if which == 0 else jnp.where(low, other, val)
    hi, lo = _split(dup)
    return jnp.where(low, hi.astype(F32), lo.astype(F32)).astype(BF)


def _stacked(val):
    return jnp.concatenate([_spread(val, 0), _spread(val, 1)], 0)


def _penalty(values):
    values = values.astype(F32)
    return GAMMA * 4.0 * values * (values * values - 1.0)


ROWS = 256
CHUNKS = tuple((i * ROWS + (AMBIT if i == 0 else 0), (i + 1) * ROWS - (AMBIT if i == 3 else 0)) for i in range(4))


def _inner_kernel(g_ref, mask_ref, bwd_ref, mid_ref, out_ref, edge_ref, rim_ref, du, staged, sem):
    mid = _dot(_stacked(g_ref[...]), mid_ref[...]).astype(BF)
    du[:64] = mid[:, :TILE]
    du[64:] = mid[:, TILE:]
    copies = []
    for i, (lo, hi) in enumerate(CHUNKS):
        rows = pl.ds(i * ROWS, ROWS)
        g = _dot(bwd_ref[rows, :], du[...]) + _penalty(mask_ref[rows, :])
        staged[rows, :] = g[:, 128:384]
        copy = pltpu.make_async_copy(
            staged.at[pl.ds(lo, hi - lo)], out_ref.at[pl.ds(lo, hi - lo), pl.ds(128, 256)], sem.at[i]
        )
        copy.start()
        copies.append(copy)
        edge_ref[rows, :128] = g[:, :128]
        edge_ref[rows, 128:] = g[:, 384:]
        if i == 0:
            rim_ref[:AMBIT] = g[:AMBIT, 128:384]
        if i == 3:
            rim_ref[AMBIT:] = g[ROWS - AMBIT :, 128:384]
    for copy in copies:
        copy.wait()


def _sides_kernel(done_ref, edge_ref, rim_ref, sa_ref, sb_ref, bwd_ref, side_ref, out_ref, part_ref, du, staged, sem):
    left, right = _by_side(sa_ref, sb_ref)
    lhs = jnp.concatenate([_stacked(left), _stacked(right)], 1)
    both = _dot(lhs, side_ref[...]).astype(BF)
    du[:64] = both[:, :128]
    du[64:] = both[:, 128:]
    low = _low_lanes((ROWS, 128))
    part_ref[:, 128:384] = rim_ref[...]
    copies = []
    for i, (lo, hi) in enumerate(CHUNKS):
        rows = pl.ds(i * ROWS, ROWS)
        g = _dot(bwd_ref[rows, :], du[...])
        for side in range(2):
            lanes = pl.ds(side * 128, 128)
            whole = edge_ref[rows, lanes] + (jnp.where(low, g, 0.0) if side == 0 else jnp.where(low, 0.0, g))
            staged[rows, lanes] = whole
            copy = pltpu.make_async_copy(
                staged.at[pl.ds(lo, hi - lo), lanes],
                out_ref.at[pl.ds(lo, hi - lo), pl.ds(side * 384, 128)],
                sem.at[2 * i + side],
            )
            copy.start()
            copies.append(copy)
            if i == 0:
                part_ref[:AMBIT, side * 384 : side * 384 + 128] = whole[:AMBIT]
            if i == 3:
                part_ref[AMBIT:, side * 384 : side * 384 + 128] = whole[ROWS - AMBIT :]
    for copy in copies:
        copy.wait()


def _rims_kernel(done_ref, part_ref, ta_ref, tb_ref, far_ref, mid_ref, side_ref, out_ref, staged, sem):
    band = lax.axis_index("own")
    even = lax.rem(band, 2) == 0
    ta = ta_ref[...].astype(F32)
    tb = jnp.where((band == 1) | (band == 2), tb_ref[...].astype(F32), 0.0)
    own, near = [], []
    for got in (jnp.where(even, tb, ta), jnp.where(even, ta, tb)):
        own.append(_spread(got[:FREQ], 0))
        near.append(jnp.concatenate([_spread(got[:FREQ], 1), _spread(got[FREQ:], 0)], 1))
    du = _dot(jnp.concatenate(own, 0), mid_ref[...])
    both = _dot(jnp.concatenate(near, 0), side_ref[...])
    low = _low_lanes((2 * FREQ, 128))
    parts = []
    for p in range(2):
        d, n = du[:, p * TILE : p * TILE + TILE], both[:, p * 128 : p * 128 + 128]
        parts.append(
            jnp.concatenate(
                [d[:, :128] + jnp.where(low, n, 0.0), d[:, 128:384], d[:, 384:] + jnp.where(low, 0.0, n)], 1
            ).astype(BF)
        )
    copies = []
    for side in range(2):
        rows = pl.ds(side * AMBIT, AMBIT)
        stack = jnp.concatenate([p[side * FREQ : side * FREQ + FREQ] for p in parts], 0)
        staged[rows, :] = part_ref[rows, :] + _dot(far_ref[rows, :], stack)
        copy = pltpu.make_async_copy(
            staged.at[rows], out_ref.at[pl.ds(side * (2 * TILE - AMBIT), AMBIT)], sem.at[side]
        )
        copy.start()
        copies.append(copy)
    for copy in copies:
        copy.wait()


def _exchange(value, target):
    bands, cols = lax.axis_size("own"), lax.axis_size("img")
    pairs = []
    for a in range(bands):
        for b in range(cols):
            c, d = target(a, b)
            pairs.append((a * cols + b, c * cols + d))
    return lax.ppermute(value, ("own", "img"), pairs)


def _img_even(a, b):
    return a, b ^ 1


def _img_odd(a, b):
    c = ((b + 1) ^ 1) - 1
    return (a, c) if 0 <= c < 32 else (a ^ 1, b)


def _own_even(a, b):
    return a ^ 1, b


def _own_odd(a, b):
    c = ((a + 1) ^ 1) - 1
    return (c, b) if 0 <= c < 4 else (a, b ^ 1)


def on_device(mask_field, target_field, occupancy, kernels, weights):
    t = {name: jnp.asarray(value) for name, value in TABLES.items()}
    vmem = pl.BlockSpec(memory_space=pltpu.VMEM)
    small = jax.ShapeDtypeStruct((FREQ, 128), F32)
    limit = lambda mib: pltpu.CompilerParams(vmem_limit_bytes=mib << 20)

    hbm = pl.BlockSpec(memory_space=pltpu.MemorySpace.HBM)
    even = lax.rem(lax.axis_index("own"), 2) == 0
    top, bottom = mask_field[:AMBIT], mask_field[2 * TILE - AMBIT :]
    ambit_a = jnp.where(even, bottom, top)
    ambit_b = jnp.where(even, top, bottom)
    halo_a = _exchange(ambit_a, _own_even)
    halo_b = _exchange(ambit_b, _own_odd)

    smem = pl.BlockSpec(memory_space=pltpu.SMEM)
    wide = jnp.sqrt(weights)[:, None, None] * kernels
    kk = jnp.concatenate([wide[0], wide[0], wide[1], wide[1]], -1)

    own, send_a, send_b = pl.pallas_call(
        _forward_kernel,
        out_shape=[small] * 3,
        in_specs=[vmem] * 8,
        out_specs=[vmem] * 3,
        scratch_shapes=[pltpu.VMEM((128, 512), BF)],
        compiler_params=limit(8),
        name="forward",
    )(mask_field, halo_a, halo_b, t["fwd"], t["fwd_ambit"], t["f_mid"], t["f_left"], t["f_right"])

    got_a = _exchange(send_a, _img_even)
    got_b = _exchange(send_b, _img_odd)

    grads = pl.pallas_call(
        _image_kernel,
        out_shape=small,
        in_specs=[vmem] * 5 + [smem] + [vmem] * 8,
        out_specs=vmem,
        scratch_shapes=[
            pltpu.VMEM((2, KERNELS, FREQ, 256), BF),
            pltpu.VMEM((KERNELS, GRID, 256), F32),
            pltpu.VMEM((2, KERNELS, FREQ, 256), BF),
            pltpu.VMEM((TILE, 128), BF),
        ],
        compiler_params=limit(24),
        name="image",
    )(
        own, got_a, got_b, kk, target_field, occupancy,
        t["tp"], t["te"], t["tx"], t["tv"], t["tz"], t["tw"], t["ty"], t["tg"],
    )

    side_a = _exchange(grads, _img_even)
    side_b = _exchange(grads, _img_odd)

    result = jax.ShapeDtypeStruct((2 * TILE, TILE), F32)
    middle, edges, rims = pl.pallas_call(
        _inner_kernel,
        out_shape=[result, jax.ShapeDtypeStruct((2 * TILE, 256), F32), jax.ShapeDtypeStruct((2 * AMBIT, 256), F32)],
        in_specs=[vmem] * 4,
        out_specs=[hbm, vmem, vmem],
        scratch_shapes=[
            pltpu.VMEM((128, TILE), BF),
            pltpu.VMEM((2 * TILE, 256), F32),
            pltpu.SemaphoreType.DMA((4,)),
        ],
        compiler_params=limit(8),
        name="inner",
    )(grads, mask_field, t["bwd"], t["b_mid"])

    pair = jax.ShapeDtypeStruct((2 * FREQ, 128), BF)
    send_a, send_b = pl.pallas_call(
        _glue_kernel,
        out_shape=[pair] * 2,
        in_specs=[vmem] * 4,
        out_specs=[vmem] * 2,
        compiler_params=limit(2),
        name="glue",
    )(rims, grads, side_a, side_b)
    tile_a = _exchange(send_a, _own_even)
    tile_b = _exchange(send_b, _own_odd)

    most, part = pl.pallas_call(
        _sides_kernel,
        out_shape=[result, jax.ShapeDtypeStruct((2 * AMBIT, TILE), F32)],
        in_specs=[hbm] + [vmem] * 6,
        out_specs=[hbm, vmem],
        scratch_shapes=[
            pltpu.VMEM((128, 128), BF),
            pltpu.VMEM((2 * TILE, 256), F32),
            pltpu.SemaphoreType.DMA((8,)),
        ],
        input_output_aliases={0: 0},
        compiler_params=limit(8),
        name="sides",
    )(middle, edges, rims, side_a, side_b, t["bwd"], t["b_side"])
    return pl.pallas_call(
        _rims_kernel,
        out_shape=result,
        in_specs=[hbm] + [vmem] * 6,
        out_specs=hbm,
        scratch_shapes=[pltpu.VMEM((2 * AMBIT, TILE), F32), pltpu.SemaphoreType.DMA((2,))],
        input_output_aliases={0: 0},
        compiler_params=limit(4),
        name="rims",
    )(most, part, tile_a, tile_b, t["far"], t["b_mid"], t["b_side"])


def solution(mesh):
    return jax.shard_map(
        on_device,
        mesh=mesh,
        in_specs=(P("own", "img"), P("own", "img"), P(), P(), P()),
        out_specs=P("own", "img"),
        check_vma=False,
    )
```
